32 devices in a mesh: wide: 4 (over z), narrow: 8 (over y, x, core).
Axes of the slice: x: 2, y: 2, z: 4, core: 2. Of those that a mesh axis runs over, the one named last changes fastest.
Arguments:
- kernel: bfloat16 [2048, 2048], P('wide', 'narrow'), may hold values from -0.15625 to 0.15625
- hamiltonian: bfloat16 [2048, 2048], P('wide', 'narrow'), may hold values from -6 to 6
- kernel_tiles: int32 [32, 32], P('wide', 'narrow'), may hold values from 0 to 1, as said below
- ham_tiles: int32 [32, 32], P('wide', 'narrow'), may hold values from 0 to 1, as said below
- pair_row: int32 [2048], P(('wide', 'narrow')), may hold values from 0 to 7
- pair_col: int32 [2048], P(('wide', 'narrow')), may hold values from 0 to 3
- sphere_phi: bfloat16 [2048, 64, 512], P(('wide', 'narrow')), may hold values from -0.09375 to 0.09375
- owner: int32 [8, 4], P('narrow'), may hold values from 0 to 3, each once within a row
Outputs:
- gradient: float32 [32, 64, 512], P(('wide', 'narrow'))
The draws below stay inside these ranges and needn't reach their ends.
Inputs may be any that keep to these rules, and one draw needn't show every extreme that they name: Each row of owner is a permutation of 0 to 3. `kernel_tiles`: in each tile row, at most 4 ones fall among one narrow index's 4 tile columns, and some row has that many. `ham_tiles`: in each tile column, at most 7 ones fall among one wide index's 8 tile rows, and some column has that many.
All inputs are finite; a program needn't handle non-finite values.
Results may differ from the reference program's by a relative error of at most 0.0029.
Values may be sent and summed in bfloat16 or wider, within the bound.
A program may use at most 128 MiB of HBM per device.

```python
import jax
import jax.numpy as jnp
from jax import lax

TILE = 64
PTS = 512
BAND = 12
PAIR_DEV = 64
DEVICES_ATOMS = 32
MAT = 2048
TR_DEV = 8
TC_DEV = 4
PAIRS = 2048
N_WIDE = 4
N_NARROW = 8
DEVICES = 32


def wire_position(tile_ids):
    return tile_ids % TR_DEV * N_WIDE + tile_ids // TR_DEV


def tile_mask(key, salt):
    base = jax.random.fold_in(key, salt)
    tile_ids = jnp.arange(DEVICES_ATOMS, dtype=jnp.int32)
    position = wire_position(tile_ids)
    spread = jnp.abs(position[:, None] - position[None, :])
    distance = jnp.minimum(spread, DEVICES_ATOMS - spread)
    coin_flip = jax.random.randint(base, (DEVICES_ATOMS, DEVICES_ATOMS), 0, 2)
    full_band = (position[:, None] % 16 == 0) | (position[None, :] % 16 == 0)
    keep_tile = (distance <= BAND - 4) | (distance <= BAND) & ((coin_flip == 1) | full_band)
    return keep_tile.astype(jnp.int32)


def draw_kernel_tiles(key, part):
    return tile_mask(key, 101)


def draw_ham_tiles(key, part):
    return tile_mask(key, 202)


def pair_draw(key):
    base = jax.random.fold_in(key, 303)
    pair_ids = jnp.arange(PAIRS, dtype=jnp.int32)
    device_ids = pair_ids // PAIR_DEV
    wide_ids = device_ids // N_NARROW
    narrow_ids = device_ids % N_NARROW
    column = jax.random.randint(jax.random.fold_in(base, 1), (PAIRS,), 0, TC_DEV)
    column_tile = narrow_ids * TC_DEV + column
    column_pos = wire_position(column_tile)
    nearest = (column_pos - wide_ids) % DEVICES_ATOMS // N_WIDE
    offset = jax.random.randint(jax.random.fold_in(base, 2), (PAIRS,), -2, 3)
    row_local = (nearest + offset) % TR_DEV
    return (row_local.astype(jnp.int32), column.astype(jnp.int32))


def draw_pair_row(key, part):
    return pair_draw(key)[0]


def draw_pair_col(key, part):
    return pair_draw(key)[1]


def shard_levels(own_key, dims, split, least, largest):
    def one(axis_at, parts):
        steps = jax.random.uniform(jax.random.fold_in(jax.random.fold_in(own_key, 6), axis_at), (parts,), jnp.float32, least / len(split), largest / len(split))
        return jnp.repeat(jnp.exp(steps), dims[axis_at] // parts).reshape((-1,) + (1,) * (len(dims) - axis_at - 1))

    level = one(*split[0])
    for cut in split[1:]:
        level = level * one(*cut)
    return level


def centred(own_key, extent, scale, bound, split=(), held_as=jnp.bfloat16):
    level = shard_levels(own_key, extent, split, -0.22, 0.18) if split else 1.0
    array = jax.random.normal(own_key, extent, jnp.float32) * scale * level
    return jnp.minimum(jnp.maximum(array, -bound), bound).astype(held_as)


def setup_inputs(seed: int = 0) -> dict:
    streams_of = jax.random.split(jax.random.key(seed), 9)
    kernel = centred(streams_of[0], (MAT, MAT), (TILE * 2 * BAND) ** -0.5, 0.15625, ((0, 4), (1, 8)))
    hamiltonian = centred(streams_of[1], (MAT, MAT), 1.0, 6.0, ((0, 4), (1, 8)))
    kernel_tiles = draw_kernel_tiles(jax.random.fold_in(streams_of[8], 71), 0)
    ham_tiles = draw_ham_tiles(jax.random.fold_in(streams_of[8], 71), 0)
    pair_row = draw_pair_row(jax.random.fold_in(streams_of[8], 71), 0)
    pair_col = draw_pair_col(jax.random.fold_in(streams_of[8], 71), 0)
    sphere_phi = centred(streams_of[6], (PAIRS, TILE, PTS), (TILE * PAIR_DEV) ** -0.5, 0.09375, ((0, 32),))
    owner = jax.vmap(lambda own: jax.random.permutation(own, TC_DEV))(jax.random.split(streams_of[7], TR_DEV)).reshape((TR_DEV, TC_DEV)).astype(jnp.int32)
    return {"kernel": kernel, "hamiltonian": hamiltonian, "kernel_tiles": kernel_tiles, "ham_tiles": ham_tiles, "pair_row": pair_row, "pair_col": pair_col, "sphere_phi": sphere_phi, "owner": owner}


def expand(mask_tiles, tile_width):
    return jnp.repeat(jnp.repeat(mask_tiles, tile_width, axis=0), tile_width, axis=1)


def reference(kernel, hamiltonian, kernel_tiles, ham_tiles, pair_row, pair_col, sphere_phi, owner):
    kmasked = kernel * expand(kernel_tiles, TILE).astype(jnp.bfloat16)
    hmasked = hamiltonian * expand(ham_tiles, TILE).astype(jnp.bfloat16)
    coefficients = jnp.dot(kmasked, hmasked, preferred_element_type=jnp.float32).astype(jnp.bfloat16)
    tile_count = MAT // TILE
    tile_table = coefficients.reshape(tile_count, TILE, tile_count, TILE).transpose(0, 2, 1, 3)
    device_ids = jnp.arange(DEVICES, dtype=jnp.int32)
    wide_ids = device_ids // N_NARROW
    narrow_ids = device_ids % N_NARROW
    row_groups = pair_row.reshape(DEVICES, PAIR_DEV)
    col_groups = pair_col.reshape(DEVICES, PAIR_DEV)
    phi_groups = sphere_phi.reshape(DEVICES, PAIR_DEV, TILE, PTS)

    def one_device(running, inputs):
        wide_id, narrow_id, rows_here, cols_here, phi_here = inputs
        block_rows = (wide_id * TR_DEV + rows_here).astype(jnp.int32)
        block_cols = (narrow_id * TC_DEV + cols_here).astype(jnp.int32)
        chosen = tile_table[block_rows, block_cols].astype(jnp.float32)
        gradient_blocks = jnp.einsum("pij,pir->pjr", chosen, phi_here.astype(jnp.float32),
                                     precision=lax.Precision.HIGHEST)
        owners = owner[narrow_id, cols_here]
        slots = (owners * N_NARROW + narrow_id).astype(jnp.int32)
        running = running + jax.ops.segment_sum(gradient_blocks, slots, num_segments=DEVICES)
        return running, None

    starting = jnp.zeros((DEVICES, TILE, PTS), jnp.float32)
    gradient, _ = lax.scan(one_device, starting, (wide_ids, narrow_ids, row_groups, col_groups, phi_groups))
    return gradient
```

```python
import functools

import jax
import jax.numpy as jnp
from jax import lax
from jax.experimental import pallas as pl
from jax.experimental.pallas import tpu as pltpu
from jax.sharding import PartitionSpec as P

MESH = pl.DeviceIdType.MESH
CHUNKS = 2
NT = (((1,), (1,)), ((), ()))


def xor(a, b, size):
    total, bit = 0, 1
    while bit < size:
        total = total + ((a // bit + b // bit) % 2) * bit
        bit *= 2
    return total


def kernel_body(
    n_wide, n_narrow, tile,
    ktiles, htiles, rows, cols, owner, k_hbm, h_hbm, phi_hbm, out_ref,
    k_in, h_in, phi, kbuf, hbuf, acc, table, lhs, own, stage, landed,
    in_sem, k_send, k_recv, s_send, s_recv, h_send, h_recv, r_send, r_recv,
):
    z = lax.axis_index("wide")
    n = lax.axis_index("narrow")
    chips = n_narrow // 2
    chip, core = n // 2, n % 2
    tile_rows, tile_cols = htiles.shape
    height, kcols = k_hbm.shape
    hrows, breadth = h_hbm.shape
    per = hrows // kcols
    width = breadth // CHUNKS
    jc = tile // CHUNKS
    pairs = rows.shape[0]
    half = width // 2

    barrier = pltpu.get_barrier_semaphore()

    def at(w, m):
        return (w, m)

    for g in range(1, chips):
        pl.semaphore_signal(barrier, inc=1, device_id=at(z, xor(chip, g, chips) * 2 + core), device_id_type=MESH)
    pl.semaphore_signal(barrier, inc=1, device_id=at(z, chip * 2 + 1 - core), device_id_type=MESH)
    for s in range(1, n_wide):
        pl.semaphore_signal(barrier, inc=1, device_id=at((z + s) % n_wide, n), device_id_type=MESH)

    load_h = pltpu.make_async_copy(h_hbm, h_in, in_sem.at[0])
    load_k = pltpu.make_async_copy(k_hbm, k_in, in_sem.at[1])
    load_p = pltpu.make_async_copy(phi_hbm, phi, in_sem.at[2])
    load_h.start()
    load_k.start()
    load_p.start()

    def mask_rows(tiles, b, extent):
        lane_tile = lax.broadcasted_iota(jnp.int32, (1, extent), 1) // tile
        mask = jnp.zeros((1, extent), jnp.float32)
        for a in range(tile_cols):
            mask = jnp.where(lane_tile == a, tiles[b, a].astype(jnp.float32), mask)
        return mask.astype(jnp.bfloat16)

    load_h.wait()
    for b in range(tile_rows):
        span = pl.ds(b * tile, tile)
        h_in[span, :] = h_in[span, :] * mask_rows(htiles, b, breadth)
    for c in range(CHUNKS):
        r = lax.broadcasted_iota(jnp.int32, (width, breadth), 0)
        col = lax.broadcasted_iota(jnp.int32, (width, breadth), 1)
        pick = (col == (r // jc) * tile + c * jc + r % jc).astype(jnp.float32).astype(jnp.bfloat16)
        hbuf[c, z] = lax.dot_general(pick, h_in[...], NT, preferred_element_type=jnp.float32).astype(jnp.bfloat16)
    load_k.wait()
    for b in range(tile_rows):
        span = pl.ds(b * tile, tile)
        kbuf[n, span, :] = k_in[span, :] * mask_rows(ktiles, b, kcols)

    pl.semaphore_wait(barrier, chips - 1 + 1 + n_wide - 1)

    def unit(u, src):
        if u == 0:
            return hbuf.at[0, src]
        return hbuf.at[1, src, pl.ds((u - 1) * half, half), :]

    def h_copy(u, way, s, src):
        ref = unit(u, src)
        return pltpu.make_async_remote_copy(
            src_ref=ref, dst_ref=ref, send_sem=h_send.at[u, way, s], recv_sem=h_recv.at[u, way, s],
            device_id=at(z + 1 if way == 0 else z - 1, n), device_id_type=MESH)

    def source(way, s):
        return z - s if way == 0 else z + s

    def has_next(way):
        return z < n_wide - 1 if way == 0 else z > 0

    def has_source(way, s):
        return z >= s if way == 0 else z < n_wide - s

    def h_start(u, way, s):
        h_copy(u, way, s, source(way, s)).start()

    def h_own(u):
        for way in range(2):
            @pl.when(has_next(way))
            def _():
                h_start(u, way, 0)

    def h_arrive(u, s):
        for way in range(2):
            @pl.when(has_source(way, s))
            def _():
                h_copy(u, way, s - 1, source(way, s)).wait_recv()
                if s < n_wide - 1:
                    @pl.when(has_next(way))
                    def _():
                        h_start(u, way, s)

    def slot(g, c):
        return kbuf.at[xor(chip, g, chips) * 2 + c]

    def k_copy(g):
        ref = slot(0, core)
        return pltpu.make_async_remote_copy(
            src_ref=ref, dst_ref=ref, send_sem=k_send.at[g], recv_sem=k_recv.at[g],
            device_id=at(z, xor(chip, g, chips) * 2 + core), device_id_type=MESH)

    def k_arrived(g):
        ref = slot(g, core)
        pltpu.make_async_remote_copy(
            src_ref=ref, dst_ref=ref, send_sem=k_send.at[g], recv_sem=k_recv.at[g],
            device_id=at(z, xor(chip, g, chips) * 2 + core), device_id_type=MESH).wait_recv()

    def sib_copy(g, c):
        ref = slot(g, c)
        return pltpu.make_async_remote_copy(
            src_ref=ref, dst_ref=ref, send_sem=s_send.at[g], recv_sem=s_recv.at[g],
            device_id=at(z, chip * 2 + 1 - core), device_id_type=MESH)

    h_own(0)
    h_own(1)
    for g in range(1, chips):
        k_copy(g).start()
    sib_copy(0, core).start()

    h_arrive(0, 1)
    h_own(2)
    for s in range(2, n_wide - 1):
        h_arrive(0, s)
    for g in range(1, chips - 1):
        k_arrived(g)
        sib_copy(g, core).start()
    h_arrive(1, 1)
    h_arrive(2, 1)
    k_arrived(chips - 1)
    sib_copy(chips - 1, core).start()
    h_arrive(0, n_wide - 1)
    for s in range(2, n_wide - 1):
        h_arrive(1, s)
        h_arrive(2, s)
    for g in range(chips):
        sib_copy(g, 1 - core).wait_recv()

    def accumulate(c, w):
        total = acc[...]
        for i in range(per):
            total = total + lax.dot_general(
                hbuf[c, w, :, i * kcols:(i + 1) * kcols], kbuf[w * per + i], NT,
                preferred_element_type=jnp.float32)
        acc[...] = total

    lane = lax.broadcasted_iota(jnp.int32, (1, 2 * tile), 1)
    low = lane < tile

    def finish(c):
        for b2 in range(tile_rows // 2):
            x = acc[:, 2 * tile * b2:2 * tile * (b2 + 1)].astype(jnp.bfloat16).astype(jnp.float32)
            y = pltpu.roll(x, tile, 1)
            for odd in range(2):
                both = jnp.where(low, x, y) if odd == 0 else jnp.where(low, y, x)
                for a in range(tile_cols):
                    table[(2 * b2 + odd) * tile_cols + a] = both[a * jc:(a + 1) * jc]

        def place(t, carry):
            c0, c1 = cols[2 * t], cols[2 * t + 1]
            first = table[rows[2 * t] * tile_cols + c0]
            second = table[rows[2 * t + 1] * tile_cols + c1]
            both = jnp.where(low, first, second)
            dest = jnp.where(low, owner[0, c0], owner[0, c1])
            at_lane = pl.ds(pl.multiple_of(t * 2 * tile, 2 * tile), 2 * tile)
            for d in range(n_wide):
                lhs[d * jc:(d + 1) * jc, at_lane] = jnp.where(dest == d, both, 0.0).astype(jnp.bfloat16)
            return carry

        lax.fori_loop(0, pairs // 2, place, 0, unroll=4)
        blocks = jnp.dot(lhs[...], phi[...], preferred_element_type=jnp.float32)
        for d in range(n_wide):
            piece = blocks[d * jc:(d + 1) * jc]
            own[c, d] = piece
            stage[c, d] = piece.astype(jnp.bfloat16)

    def r_copy(c, s):
        return pltpu.make_async_remote_copy(
            src_ref=stage.at[c, (z + s) % n_wide], dst_ref=landed.at[c, s - 1],
            send_sem=r_send.at[c, s - 1], recv_sem=r_recv.at[c, s - 1],
            device_id=at((z + s) % n_wide, n), device_id_type=MESH)

    def loop(c, lo, hi):
        acc[...] = jnp.zeros_like(acc)

        def step(w, carry):
            accumulate(c, w)
            return carry

        lax.fori_loop(lo, hi, step, 0)

    load_p.wait()
    loop(0, 0, n_wide)
    finish(0)
    for s in range(1, n_wide):
        r_copy(0, s).start()
    loop(1, z // (n_wide - 1), n_wide - (n_wide - 1 - z) // (n_wide - 1))
    h_arrive(1, n_wide - 1)
    h_arrive(2, n_wide - 1)

    @pl.when(z == 0)
    def _():
        accumulate(1, n_wide - 1)

    @pl.when(z == n_wide - 1)
    def _():
        accumulate(1, 0)

    finish(1)
    for s in range(1, n_wide):
        r_copy(1, s).start()

    for c in range(CHUNKS):
        total = own[c, z]
        for s in range(1, n_wide):
            r_copy(c, s).wait_recv()
            total = total + landed[c, s - 1].astype(jnp.float32)
        out_ref[0, c * jc:(c + 1) * jc, :] = total

    for c in range(CHUNKS):
        for s in range(1, n_wide):
            r_copy(c, s).wait_send()
    for g in range(1, chips):
        k_copy(g).wait_send()
    for g in range(chips):
        sib_copy(g, core).wait_send()
    for u in range(3):
        for way in range(2):
            for s in range(n_wide - 1):
                @pl.when(has_next(way) & has_source(way, s))
                def _():
                    h_copy(u, way, s, source(way, s)).wait_send()


def body(n_wide, n_narrow, kernel, hamiltonian, kernel_tiles, ham_tiles, pair_row, pair_col, sphere_phi, owner):
    pairs, tile, pts = sphere_phi.shape
    height, kcols = kernel.shape
    hrows, breadth = hamiltonian.shape
    tile_rows, tile_cols = ham_tiles.shape
    width, jc = breadth // CHUNKS, tile // CHUNKS
    chips = n_narrow // 2
    smem = pl.BlockSpec(memory_space=pltpu.SMEM)
    hbm = pl.BlockSpec(memory_space=pl.ANY)
    dma = pltpu.SemaphoreType.DMA
    return pl.pallas_call(
        functools.partial(kernel_body, n_wide, n_narrow, tile),
        out_shape=jax.ShapeDtypeStruct((1, tile, pts), jnp.float32),
        in_specs=[smem] * 5 + [hbm] * 3,
        out_specs=pl.BlockSpec(memory_space=pltpu.VMEM),
        scratch_shapes=[
            pltpu.VMEM((height, kcols), jnp.bfloat16),
            pltpu.VMEM((hrows, breadth), jnp.bfloat16),
            pltpu.VMEM((pairs * tile, pts), jnp.bfloat16),
            pltpu.VMEM((n_narrow, height, kcols), jnp.bfloat16),
            pltpu.VMEM((CHUNKS, n_wide, width, hrows), jnp.bfloat16),
            pltpu.VMEM((width, height), jnp.float32),
            pltpu.VMEM((tile_rows * tile_cols, jc, 2 * tile), jnp.float32),
            pltpu.VMEM((n_wide * jc, pairs * tile), jnp.bfloat16),
            pltpu.VMEM((CHUNKS, n_wide, jc, pts), jnp.float32),
            pltpu.VMEM((CHUNKS, n_wide, jc, pts), jnp.bfloat16),
            pltpu.VMEM((CHUNKS, n_wide - 1, jc, pts), jnp.bfloat16),
            dma((3,)),
            dma((chips,)), dma((chips,)),
            dma((chips,)), dma((chips,)),
            dma((3, 2, n_wide)), dma((3, 2, n_wide)),
            dma((CHUNKS, n_wide)), dma((CHUNKS, n_wide)),
        ],
        compiler_params=pltpu.CompilerParams(
            collective_id=0, has_side_effects=True, vmem_limit_bytes=60 * 2**20),
    )(kernel_tiles, ham_tiles, pair_row, pair_col, owner, kernel, hamiltonian,
      sphere_phi.reshape(pairs * tile, pts))


def solution(mesh):
    return jax.shard_map(
        functools.partial(body, mesh.shape["wide"], mesh.shape["narrow"]),
        mesh=mesh,
        in_specs=(
            P("wide", "narrow"),
            P("wide", "narrow"),
            P("wide", "narrow"),
            P("wide", "narrow"),
            P(("wide", "narrow")),
            P(("wide", "narrow")),
            P(("wide", "narrow"), None, None),
            P("narrow", None),
        ),
        out_specs=P(("wide", "narrow"), None, None),
        check_vma=False,
    )
```

```python
import functools

import jax
import jax.numpy as jnp
from jax import lax
from jax.experimental import pallas as pl
from jax.experimental.pallas import tpu as pltpu
from jax.sharding import PartitionSpec as P

MESH = pl.DeviceIdType.MESH
CHUNKS = 2
NT = (((1,), (1,)), ((), ()))


def xor(a, b, size):
    total, bit = 0, 1
    while bit < size:
        total = total + ((a // bit + b // bit) % 2) * bit
        bit *= 2
    return total


def kernel_body(
    n_wide, n_narrow, tile,
    ktiles, htiles, rows, cols, owner, k_hbm, h_hbm, phi_hbm, out_ref,
    k_in, h_in, phi, kbuf, hbuf, acc, table, lhs, own, stage, landed,
    in_sem, k_send, k_recv, s_send, s_recv, h_send, h_recv, r_send, r_recv,
):
    z = lax.axis_index("wide")
    n = lax.axis_index("narrow")
    chips = n_narrow // 2
    chip, core = n // 2, n % 2
    tile_cols, tile_rows = htiles.shape
    height, kcols = k_hbm.shape
    hrows, breadth = h_hbm.shape
    per = hrows // kcols
    width = breadth // CHUNKS
    jc = tile // CHUNKS
    pairs = rows.shape[0]
    half = width // 2

    barrier = pltpu.get_barrier_semaphore()

    def at(w, m):
        return (w, m)

    for g in range(1, chips):
        pl.semaphore_signal(barrier, inc=1, device_id=at(z, xor(chip, g, chips) * 2 + core), device_id_type=MESH)
    pl.semaphore_signal(barrier, inc=1, device_id=at(z, chip * 2 + 1 - core), device_id_type=MESH)
    for s in range(1, n_wide):
        pl.semaphore_signal(barrier, inc=1, device_id=at((z + s) % n_wide, n), device_id_type=MESH)

    load_h = pltpu.make_async_copy(h_hbm, h_in, in_sem.at[0])
    load_k = pltpu.make_async_copy(k_hbm, k_in, in_sem.at[1])
    load_p = pltpu.make_async_copy(phi_hbm, phi, in_sem.at[2])
    load_h.start()
    load_k.start()
    load_p.start()

    def mask_rows(tiles, b, extent):
        lane_tile = lax.broadcasted_iota(jnp.int32, (1, extent), 1) // tile
        mask = jnp.zeros((1, extent), jnp.float32)
        for a in range(tile_cols):
            mask = jnp.where(lane_tile == a, tiles[a, b].astype(jnp.float32), mask)
        return mask.astype(jnp.bfloat16)

    load_h.wait()
    for b in range(tile_rows):
        span = pl.ds(b * tile, tile)
        h_in[span, :] = h_in[span, :] * mask_rows(htiles, b, breadth)
    for c in range(CHUNKS):
        r = lax.broadcasted_iota(jnp.int32, (width, breadth), 0)
        col = lax.broadcasted_iota(jnp.int32, (width, breadth), 1)
        pick = (col == (r // jc) * tile + c * jc + r % jc).astype(jnp.float32).astype(jnp.bfloat16)
        hbuf[c, z] = lax.dot_general(pick, h_in[...], NT, preferred_element_type=jnp.float32).astype(jnp.bfloat16)
    pl.semaphore_wait(barrier, chips - 1 + 1 + n_wide - 1)

    def unit(u, src):
        if u == 0:
            return hbuf.at[0, src]
        return hbuf.at[1, src, pl.ds((u - 1) * half, half), :]

    def h_copy(u, way, s, src):
        ref = unit(u, src)
        return pltpu.make_async_remote_copy(
            src_ref=ref, dst_ref=ref, send_sem=h_send.at[u, way, s], recv_sem=h_recv.at[u, way, s],
            device_id=at(z + 1 if way == 0 else z - 1, n), device_id_type=MESH)

    def source(way, s):
        return z - s if way == 0 else z + s

    def has_next(way):
        return z < n_wide - 1 if way == 0 else z > 0

    def has_source(way, s):
        return z >= s if way == 0 else z < n_wide - s

    def h_start(u, way, s):
        h_copy(u, way, s, source(way, s)).start()

    def h_own(u):
        for way in range(2):
            @pl.when(has_next(way))
            def _():
                h_start(u, way, 0)

    def h_arrive(u, s):
        for way in range(2):
            @pl.when(has_source(way, s))
            def _():
                h_copy(u, way, s - 1, source(way, s)).wait_recv()
                if s < n_wide - 1:
                    @pl.when(has_next(way))
                    def _():
                        h_start(u, way, s)

    def slot(g, c):
        return kbuf.at[xor(chip, g, chips) * 2 + c]

    def k_copy(g):
        ref = slot(0, core)
        return pltpu.make_async_remote_copy(
            src_ref=ref, dst_ref=ref, send_sem=k_send.at[g], recv_sem=k_recv.at[g],
            device_id=at(z, xor(chip, g, chips) * 2 + core), device_id_type=MESH)

    def k_arrived(g):
        ref = slot(g, core)
        pltpu.make_async_remote_copy(
            src_ref=ref, dst_ref=ref, send_sem=k_send.at[g], recv_sem=k_recv.at[g],
            device_id=at(z, xor(chip, g, chips) * 2 + core), device_id_type=MESH).wait_recv()

    def sib_copy(g, c):
        ref = slot(g, c)
        return pltpu.make_async_remote_copy(
            src_ref=ref, dst_ref=ref, send_sem=s_send.at[g], recv_sem=s_recv.at[g],
            device_id=at(z, chip * 2 + 1 - core), device_id_type=MESH)

    h_own(0)
    h_own(1)
    load_k.wait()
    for b in range(tile_rows):
        span = pl.ds(b * tile, tile)
        kbuf[n, span, :] = k_in[span, :] * mask_rows(ktiles, b, kcols)
    for g in range(1, chips):
        k_copy(g).start()
    sib_copy(0, core).start()

    h_arrive(0, 1)
    h_own(2)
    for s in range(2, n_wide - 1):
        h_arrive(0, s)
    for g in range(1, chips - 1):
        k_arrived(g)
        sib_copy(g, core).start()
    h_arrive(1, 1)
    h_arrive(2, 1)
    k_arrived(chips - 1)
    sib_copy(chips - 1, core).start()
    h_arrive(0, n_wide - 1)
    for s in range(2, n_wide - 1):
        h_arrive(1, s)
        h_arrive(2, s)
    for g in range(chips):
        sib_copy(g, 1 - core).wait_recv()

    def accumulate(c, w):
        total = acc[...]
        for i in range(per):
            total = total + lax.dot_general(
                hbuf[c, w, :, i * kcols:(i + 1) * kcols], kbuf[w * per + i], NT,
                preferred_element_type=jnp.float32)
        acc[...] = total

    lane = lax.broadcasted_iota(jnp.int32, (1, 2 * tile), 1)
    low = lane < tile

    def finish(c):
        for b2 in range(tile_rows // 2):
            x = acc[:, 2 * tile * b2:2 * tile * (b2 + 1)].astype(jnp.bfloat16).astype(jnp.float32)
            y = pltpu.roll(x, tile, 1)
            for odd in range(2):
                both = jnp.where(low, x, y) if odd == 0 else jnp.where(low, y, x)
                for a in range(tile_cols):
                    table[(2 * b2 + odd) * tile_cols + a] = both[a * jc:(a + 1) * jc]

        def place(t, carry):
            c0, c1 = cols[2 * t], cols[2 * t + 1]
            first = table[rows[2 * t] * tile_cols + c0]
            second = table[rows[2 * t + 1] * tile_cols + c1]
            both = jnp.where(low, first, second)
            dest = jnp.where(low, owner[0, c0], owner[0, c1])
            at_lane = pl.ds(pl.multiple_of(t * 2 * tile, 2 * tile), 2 * tile)
            for d in range(n_wide):
                lhs[d * jc:(d + 1) * jc, at_lane] = jnp.where(dest == d, both, 0.0).astype(jnp.bfloat16)
            return carry

        lax.fori_loop(0, pairs // 2, place, 0, unroll=4)
        blocks = jnp.dot(lhs[...], phi[...], preferred_element_type=jnp.float32)
        for d in range(n_wide):
            piece = blocks[d * jc:(d + 1) * jc]
            own[c, d] = piece
            stage[c, d] = piece.astype(jnp.bfloat16)

    def r_copy(c, s):
        return pltpu.make_async_remote_copy(
            src_ref=stage.at[c, (z + s) % n_wide], dst_ref=landed.at[c, s - 1],
            send_sem=r_send.at[c, s - 1], recv_sem=r_recv.at[c, s - 1],
            device_id=at((z + s) % n_wide, n), device_id_type=MESH)

    def loop(c, lo, hi):
        acc[...] = jnp.zeros_like(acc)

        def step(w, carry):
            accumulate(c, w)
            return carry

        lax.fori_loop(lo, hi, step, 0)

    load_p.wait()
    loop(0, 0, n_wide)
    finish(0)
    for s in range(1, n_wide):
        r_copy(0, s).start()
    loop(1, z // (n_wide - 1), n_wide - (n_wide - 1 - z) // (n_wide - 1))
    h_arrive(1, n_wide - 1)
    h_arrive(2, n_wide - 1)

    @pl.when(z == 0)
    def _():
        accumulate(1, n_wide - 1)

    @pl.when(z == n_wide - 1)
    def _():
        accumulate(1, 0)

    finish(1)
    for s in range(1, n_wide):
        r_copy(1, s).start()

    for c in range(CHUNKS):
        total = own[c, z]
        for s in range(1, n_wide):
            r_copy(c, s).wait_recv()
            total = total + landed[c, s - 1].astype(jnp.float32)
        out_ref[0, c * jc:(c + 1) * jc, :] = total

    for c in range(CHUNKS):
        for s in range(1, n_wide):
            r_copy(c, s).wait_send()
    for g in range(1, chips):
        k_copy(g).wait_send()
    for g in range(chips):
        sib_copy(g, core).wait_send()
    for u in range(3):
        for way in range(2):
            for s in range(n_wide - 1):
                @pl.when(has_next(way) & has_source(way, s))
                def _():
                    h_copy(u, way, s, source(way, s)).wait_send()


def body(n_wide, n_narrow, kernel, hamiltonian, kernel_tiles, ham_tiles, pair_row, pair_col, sphere_phi, owner):
    pairs, tile, pts = sphere_phi.shape
    height, kcols = kernel.shape
    hrows, breadth = hamiltonian.shape
    tile_rows, tile_cols = ham_tiles.shape
    width, jc = breadth // CHUNKS, tile // CHUNKS
    chips = n_narrow // 2
    smem = pl.BlockSpec(memory_space=pltpu.SMEM)
    hbm = pl.BlockSpec(memory_space=pltpu.HBM)
    dma = pltpu.SemaphoreType.DMA
    return pl.pallas_call(
        functools.partial(kernel_body, n_wide, n_narrow, tile),
        out_shape=jax.ShapeDtypeStruct((1, tile, pts), jnp.float32),
        in_specs=[smem] * 5 + [hbm] * 3,
        out_specs=pl.BlockSpec(memory_space=pltpu.VMEM),
        scratch_shapes=[
            pltpu.VMEM((height, kcols), jnp.bfloat16),
            pltpu.VMEM((hrows, breadth), jnp.bfloat16),
            pltpu.VMEM((pairs * tile, pts), jnp.bfloat16),
            pltpu.VMEM((n_narrow, height, kcols), jnp.bfloat16),
            pltpu.VMEM((CHUNKS, n_wide, width, hrows), jnp.bfloat16),
            pltpu.VMEM((width, height), jnp.float32),
            pltpu.VMEM((tile_rows * tile_cols, jc, 2 * tile), jnp.float32),
            pltpu.VMEM((n_wide * jc, pairs * tile), jnp.bfloat16),
            pltpu.VMEM((CHUNKS, n_wide, jc, pts), jnp.float32),
            pltpu.VMEM((CHUNKS, n_wide, jc, pts), jnp.bfloat16),
            pltpu.VMEM((CHUNKS, n_wide - 1, jc, pts), jnp.bfloat16),
            dma((3,)),
            dma((chips,)), dma((chips,)),
            dma((chips,)), dma((chips,)),
            dma((3, 2, n_wide)), dma((3, 2, n_wide)),
            dma((CHUNKS, n_wide)), dma((CHUNKS, n_wide)),
        ],
        compiler_params=pltpu.CompilerParams(
            collective_id=0, has_side_effects=True, vmem_limit_bytes=60 * 2**20),
    )(kernel_tiles.T, ham_tiles.T, pair_row, pair_col, owner, kernel, hamiltonian,
      sphere_phi.reshape(pairs * tile, pts))


def solution(mesh):
    return jax.shard_map(
        functools.partial(body, mesh.shape["wide"], mesh.shape["narrow"]),
        mesh=mesh,
        in_specs=(
            P("wide", "narrow"),
            P("wide", "narrow"),
            P("wide", "narrow"),
            P("wide", "narrow"),
            P(("wide", "narrow")),
            P(("wide", "narrow")),
            P(("wide", "narrow"), None, None),
            P("narrow", None),
        ),
        out_specs=P(("wide", "narrow"), None, None),
        check_vma=False,
    )
```

```python
import functools

import jax
import jax.numpy as jnp
from jax import lax
from jax.experimental import pallas as pl
from jax.experimental.pallas import tpu as pltpu
from jax.sharding import PartitionSpec as P

MESH = pl.DeviceIdType.MESH
CHUNKS = 2
NT = (((1,), (1,)), ((), ()))


def xor(a, b, size):
    total, bit = 0, 1
    while bit < size:
        total = total + ((a // bit + b // bit) % 2) * bit
        bit *= 2
    return total


def kernel_body(
    n_wide, n_narrow, tile,
    ktiles_hbm, htiles_hbm, rows_hbm, cols_hbm, owner_hbm, k_hbm, h_hbm, phi_hbm, out_ref,
    ktiles, htiles, rows, cols, owner, k_in, h_in, phi, kbuf, hbuf, acc, table, lhs, own, stage, landed,
    in_sem, k_send, k_recv, s_send, s_recv, h_send, h_recv, r_send, r_recv,
):
    z = lax.axis_index("wide")
    n = lax.axis_index("narrow")
    chips = n_narrow // 2
    chip, core = n // 2, n % 2
    tile_cols, tile_rows = htiles.shape
    height, kcols = k_hbm.shape
    hrows, breadth = h_hbm.shape
    per = hrows // kcols
    width = breadth // CHUNKS
    jc = tile // CHUNKS
    pairs = rows.shape[0]
    half = width // 2

    barrier = pltpu.get_barrier_semaphore()

    def at(w, m):
        return (w, m)

    for g in range(1, chips):
        pl.semaphore_signal(barrier, inc=1, device_id=at(z, xor(chip, g, chips) * 2 + core), device_id_type=MESH)
    pl.semaphore_signal(barrier, inc=1, device_id=at(z, chip * 2 + 1 - core), device_id_type=MESH)
    for s in range(1, n_wide):
        pl.semaphore_signal(barrier, inc=1, device_id=at((z + s) % n_wide, n), device_id_type=MESH)

    load_h = pltpu.make_async_copy(h_hbm, h_in, in_sem.at[0])
    load_k = pltpu.make_async_copy(k_hbm, k_in, in_sem.at[1])
    load_p = pltpu.make_async_copy(phi_hbm, phi, in_sem.at[2])
    tables = [
        pltpu.make_async_copy(a, b, in_sem.at[3 + i])
        for i, (a, b) in enumerate((
            (htiles_hbm, htiles), (ktiles_hbm, ktiles), (rows_hbm, rows), (cols_hbm, cols), (owner_hbm, owner)))
    ]
    tables[0].start()
    load_h.start()
    load_k.start()
    for load in tables[1:]:
        load.start()
    load_p.start()

    def mask_rows(tiles, b, extent):
        lane_tile = lax.broadcasted_iota(jnp.int32, (1, extent), 1) // tile
        mask = jnp.zeros((1, extent), jnp.float32)
        for a in range(tile_cols):
            mask = jnp.where(lane_tile == a, tiles[a, b].astype(jnp.float32), mask)
        return mask.astype(jnp.bfloat16)

    tables[0].wait()
    load_h.wait()
    for b in range(tile_rows):
        span = pl.ds(b * tile, tile)
        h_in[span, :] = h_in[span, :] * mask_rows(htiles, b, breadth)
    for c in range(CHUNKS):
        r = lax.broadcasted_iota(jnp.int32, (width, breadth), 0)
        col = lax.broadcasted_iota(jnp.int32, (width, breadth), 1)
        pick = (col == (r // jc) * tile + c * jc + r % jc).astype(jnp.float32).astype(jnp.bfloat16)
        hbuf[c, z] = lax.dot_general(pick, h_in[...], NT, preferred_element_type=jnp.float32).astype(jnp.bfloat16)
    pl.semaphore_wait(barrier, chips - 1 + 1 + n_wide - 1)

    def unit(u, src):
        if u == 0:
            return hbuf.at[0, src]
        return hbuf.at[1, src, pl.ds((u - 1) * half, half), :]

    def h_copy(u, way, s, src):
        ref = unit(u, src)
        return pltpu.make_async_remote_copy(
            src_ref=ref, dst_ref=ref, send_sem=h_send.at[u, way, s], recv_sem=h_recv.at[u, way, s],
            device_id=at(z + 1 if way == 0 else z - 1, n), device_id_type=MESH)

    def source(way, s):
        return z - s if way == 0 else z + s

    def has_next(way):
        return z < n_wide - 1 if way == 0 else z > 0

    def has_source(way, s):
        return z >= s if way == 0 else z < n_wide - s

    def h_start(u, way, s):
        h_copy(u, way, s, source(way, s)).start()

    def h_own(u):
        for way in range(2):
            @pl.when(has_next(way))
            def _():
                h_start(u, way, 0)

    def h_arrive(u, s):
        for way in range(2):
            @pl.when(has_source(way, s))
            def _():
                h_copy(u, way, s - 1, source(way, s)).wait_recv()
                if s < n_wide - 1:
                    @pl.when(has_next(way))
                    def _():
                        h_start(u, way, s)

    def slot(g, c):
        return kbuf.at[xor(chip, g, chips) * 2 + c]

    def k_copy(g):
        ref = slot(0, core)
        return pltpu.make_async_remote_copy(
            src_ref=ref, dst_ref=ref, send_sem=k_send.at[g], recv_sem=k_recv.at[g],
            device_id=at(z, xor(chip, g, chips) * 2 + core), device_id_type=MESH)

    def k_arrived(g):
        ref = slot(g, core)
        pltpu.make_async_remote_copy(
            src_ref=ref, dst_ref=ref, send_sem=k_send.at[g], recv_sem=k_recv.at[g],
            device_id=at(z, xor(chip, g, chips) * 2 + core), device_id_type=MESH).wait_recv()

    def sib_copy(g, c):
        ref = slot(g, c)
        return pltpu.make_async_remote_copy(
            src_ref=ref, dst_ref=ref, send_sem=s_send.at[g], recv_sem=s_recv.at[g],
            device_id=at(z, chip * 2 + 1 - core), device_id_type=MESH)

    h_own(0)
    h_own(1)
    tables[1].wait()
    load_k.wait()
    for b in range(tile_rows):
        span = pl.ds(b * tile, tile)
        kbuf[n, span, :] = k_in[span, :] * mask_rows(ktiles, b, kcols)
    for g in range(1, chips):
        k_copy(g).start()
    sib_copy(0, core).start()

    h_own(2)
    h_arrive(0, 1)
    h_arrive(1, 1)
    h_arrive(2, 1)
    for s in range(2, n_wide - 1):
        h_arrive(0, s)
    for g in range(1, chips - 1):
        k_arrived(g)
        sib_copy(g, core).start()
    for s in range(2, n_wide - 1):
        h_arrive(1, s)
    k_arrived(chips - 1)
    sib_copy(chips - 1, core).start()
    h_arrive(0, n_wide - 1)
    for s in range(2, n_wide - 1):
        h_arrive(2, s)
    for g in range(chips):
        sib_copy(g, 1 - core).wait_recv()

    def accumulate(c, w):
        total = acc[...]
        for i in range(per):
            total = total + lax.dot_general(
                hbuf[c, w, :, i * kcols:(i + 1) * kcols], kbuf[w * per + i], NT,
                preferred_element_type=jnp.float32)
        acc[...] = total

    lane = lax.broadcasted_iota(jnp.int32, (1, 2 * tile), 1)
    low = lane < tile

    def finish(c):
        for b2 in range(tile_rows // 2):
            x = acc[:, 2 * tile * b2:2 * tile * (b2 + 1)].astype(jnp.bfloat16).astype(jnp.float32)
            y = pltpu.roll(x, tile, 1)
            for odd in range(2):
                both = jnp.where(low, x, y) if odd == 0 else jnp.where(low, y, x)
                for a in range(tile_cols):
                    table[(2 * b2 + odd) * tile_cols + a] = both[a * jc:(a + 1) * jc]

        def place(t, carry):
            c0, c1 = cols[2 * t], cols[2 * t + 1]
            first = table[rows[2 * t] * tile_cols + c0]
            second = table[rows[2 * t + 1] * tile_cols + c1]
            both = jnp.where(low, first, second)
            dest = jnp.where(low, owner[0, c0], owner[0, c1])
            at_lane = pl.ds(pl.multiple_of(t * 2 * tile, 2 * tile), 2 * tile)
            for d in range(n_wide):
                lhs[d * jc:(d + 1) * jc, at_lane] = jnp.where(dest == d, both, 0.0).astype(jnp.bfloat16)
            return carry

        lax.fori_loop(0, pairs // 2, place, 0, unroll=4)
        blocks = jnp.dot(lhs[...], phi[...], preferred_element_type=jnp.float32)
        for d in range(n_wide):
            piece = blocks[d * jc:(d + 1) * jc]
            own[c, d] = piece
            stage[c, d] = piece.astype(jnp.bfloat16)

    def r_copy(c, s):
        return pltpu.make_async_remote_copy(
            src_ref=stage.at[c, (z + s) % n_wide], dst_ref=landed.at[c, s - 1],
            send_sem=r_send.at[c, s - 1], recv_sem=r_recv.at[c, s - 1],
            device_id=at((z + s) % n_wide, n), device_id_type=MESH)

    def loop(c, lo, hi):
        acc[...] = jnp.zeros_like(acc)

        def step(w, carry):
            accumulate(c, w)
            return carry

        lax.fori_loop(lo, hi, step, 0)

    load_p.wait()
    for load in tables[2:]:
        load.wait()
    loop(0, 0, n_wide)
    finish(0)
    for s in range(1, n_wide):
        r_copy(0, s).start()
    loop(1, z // (n_wide - 1), n_wide - (n_wide - 1 - z) // (n_wide - 1))
    h_arrive(1, n_wide - 1)
    h_arrive(2, n_wide - 1)

    @pl.when(z == 0)
    def _():
        accumulate(1, n_wide - 1)

    @pl.when(z == n_wide - 1)
    def _():
        accumulate(1, 0)

    finish(1)
    for s in range(1, n_wide):
        r_copy(1, s).start()

    for c in range(CHUNKS):
        total = own[c, z]
        for s in range(1, n_wide):
            r_copy(c, s).wait_recv()
            total = total + landed[c, s - 1].astype(jnp.float32)
        out_ref[0, c * jc:(c + 1) * jc, :] = total

    for c in range(CHUNKS):
        for s in range(1, n_wide):
            r_copy(c, s).wait_send()
    for g in range(1, chips):
        k_copy(g).wait_send()
    for g in range(chips):
        sib_copy(g, core).wait_send()
    for u in range(3):
        for way in range(2):
            for s in range(n_wide - 1):
                @pl.when(has_next(way) & has_source(way, s))
                def _():
                    h_copy(u, way, s, source(way, s)).wait_send()


def body(n_wide, n_narrow, kernel, hamiltonian, kernel_tiles, ham_tiles, pair_row, pair_col, sphere_phi, owner):
    pairs, tile, pts = sphere_phi.shape
    height, kcols = kernel.shape
    hrows, breadth = hamiltonian.shape
    tile_rows, tile_cols = ham_tiles.shape
    width, jc = breadth // CHUNKS, tile // CHUNKS
    chips = n_narrow // 2
    hbm = pl.BlockSpec(memory_space=pltpu.HBM)
    dma = pltpu.SemaphoreType.DMA
    return pl.pallas_call(
        functools.partial(kernel_body, n_wide, n_narrow, tile),
        out_shape=jax.ShapeDtypeStruct((1, tile, pts), jnp.float32),
        in_specs=[hbm] * 8,
        out_specs=pl.BlockSpec(memory_space=pltpu.VMEM),
        scratch_shapes=[
            pltpu.SMEM((tile_cols, tile_rows), jnp.int32),
            pltpu.SMEM((tile_cols, tile_rows), jnp.int32),
            pltpu.SMEM((pairs,), jnp.int32),
            pltpu.SMEM((pairs,), jnp.int32),
            pltpu.SMEM((1, tile_cols), jnp.int32),
            pltpu.VMEM((height, kcols), jnp.bfloat16),
            pltpu.VMEM((hrows, breadth), jnp.bfloat16),
            pltpu.VMEM((pairs * tile, pts), jnp.bfloat16),
            pltpu.VMEM((n_narrow, height, kcols), jnp.bfloat16),
            pltpu.VMEM((CHUNKS, n_wide, width, hrows), jnp.bfloat16),
            pltpu.VMEM((width, height), jnp.float32),
            pltpu.VMEM((tile_rows * tile_cols, jc, 2 * tile), jnp.float32),
            pltpu.VMEM((n_wide * jc, pairs * tile), jnp.bfloat16),
            pltpu.VMEM((CHUNKS, n_wide, jc, pts), jnp.float32),
            pltpu.VMEM((CHUNKS, n_wide, jc, pts), jnp.bfloat16),
            pltpu.VMEM((CHUNKS, n_wide - 1, jc, pts), jnp.bfloat16),
            dma((8,)),
            dma((chips,)), dma((chips,)),
            dma((chips,)), dma((chips,)),
            dma((3, 2, n_wide)), dma((3, 2, n_wide)),
            dma((CHUNKS, n_wide)), dma((CHUNKS, n_wide)),
        ],
        compiler_params=pltpu.CompilerParams(
            collective_id=0, has_side_effects=True, vmem_limit_bytes=60 * 2**20),
    )(kernel_tiles.T, ham_tiles.T, pair_row, pair_col, owner, kernel, hamiltonian,
      sphere_phi.reshape(pairs * tile, pts))


def solution(mesh):
    return jax.shard_map(
        functools.partial(body, mesh.shape["wide"], mesh.shape["narrow"]),
        mesh=mesh,
        in_specs=(
            P("wide", "narrow"),
            P("wide", "narrow"),
            P("wide", "narrow"),
            P("wide", "narrow"),
            P(("wide", "narrow")),
            P(("wide", "narrow")),
            P(("wide", "narrow"), None, None),
            P("narrow", None),
        ),
        out_specs=P(("wide", "narrow"), None, None),
        check_vma=False,
    )
```
